256 devices in a mesh: space: 32 (over x, z_hi, y), ens: 8 (over z_lo, core).
Axes of the slice: x: 4, y: 4, z: 8 (z_hi: 2, z_lo: 4; z = z_hi * 4 + z_lo), core: 2. Of those that a mesh axis runs over, the one named last changes fastest.
Arguments:
- outlook_array: bfloat16 [1536, 49152], P('ens', 'space'), may hold values from -57 to 57
- earlier_location_basis: bfloat16 [49152, 256], P('space'), may hold values from -4 to 4
- earlier_ensemble_basis: float32 [48, 16], replicated, may hold values from -4 to 4
- earlier_height_basis: float32 [32, 16], replicated, may hold values from -4 to 4
Outputs:
- spatial_factor: float32 [49152, 256], P(('space', 'ens'))
- member_factor: float32 [48, 16], replicated
- level_factor: float32 [32, 16], replicated
The draws below stay inside these ranges and needn't reach their ends.
All inputs are finite; a program needn't handle non-finite values.
Results may differ from the reference program's by a relative error of at most 0.0075.
The reference program's roundings to bfloat16 on the way count: a program that leaves them out, or rounds other values in their place, can miss the bound.
Values may be sent and summed in bfloat16 or wider, within the bound.
A program may use at most 64 MiB of HBM per device.

```python
import jax
import jax.numpy as jnp
from jax import lax

MEMBERS = 48
LEVELS = 32
RANK = 256
MEMBER_RANK = 16
LEVEL_RANK = 16
PASSES = 3
GRID = 49152


def draw_outlook_array(key, part):
    subkeys = jax.random.split(jax.random.fold_in(key, 11), 7)
    shared = jnp.clip(jax.random.normal(subkeys[0], (1, 1, GRID), jnp.float32), -4.0, 4.0)
    own_field = jnp.clip(jax.random.normal(subkeys[1], (LEVELS, 1, GRID), jnp.float32), -4.0, 4.0)
    member_noise = jnp.clip(jax.random.normal(subkeys[2], (LEVELS, MEMBERS, GRID), jnp.float32), -4.0, 4.0)
    level_mix = jax.random.uniform(subkeys[3], (LEVELS, 1, 1), jnp.float32, -1.5, 1.5)
    level_scale = jnp.exp(jax.random.uniform(subkeys[4], (LEVELS, 1, 1), jnp.float32, -0.7, 0.7))
    member_scale = jnp.exp(jax.random.uniform(subkeys[5], (1, MEMBERS, 1), jnp.float32, -0.7, 0.4))
    position = jnp.arange(GRID, dtype=jnp.float32).reshape(1, 1, GRID) / GRID
    ramp = jnp.exp(1.2 * (position - 1.0))
    grid_scale = ramp * jnp.exp(jax.random.uniform(subkeys[6], (1, 1, GRID), jnp.float32, -0.7, 0.7))
    mean_field = level_mix * shared + own_field
    values = level_scale * grid_scale * (0.8 * mean_field + member_scale * member_noise)
    return values.reshape(LEVELS * MEMBERS, GRID).astype(jnp.bfloat16)


def block_scale(key, dims, shards, smallest, top_value):
    factor_of = 1.0
    for dim, blocks in shards:
        heights = jax.random.uniform(jax.random.fold_in(jax.random.fold_in(key, 6), dim), (blocks,), jnp.float32, smallest / len(shards), top_value / len(shards))
        factor_of = factor_of * jnp.repeat(jnp.exp(heights), dims[dim] // blocks).reshape((-1,) + (1,) * (len(dims) - 1 - dim))
    return factor_of


def gaussian(own_key, dims, spread, most, cuts=(), held_as=jnp.bfloat16):
    factor_of = block_scale(own_key, dims, cuts, -0.22, 0.18) if cuts else 1.0
    values = jax.random.normal(own_key, dims, jnp.float32) * spread * factor_of
    return jnp.minimum(jnp.maximum(values, -most), most).astype(held_as)


def setup_inputs(seed: int = 0) -> dict:
    splits = jax.random.split(jax.random.key(seed), 5)
    return {
        "outlook_array": draw_outlook_array(jax.random.fold_in(splits[4], 71), 0),
        "earlier_location_basis": gaussian(splits[1], (GRID, RANK), 1.0, 4.0, ((0, 32),)),
        "earlier_ensemble_basis": gaussian(splits[2], (MEMBERS, MEMBER_RANK), 1.0, 4.0, (), jnp.float32),
        "earlier_height_basis": gaussian(splits[3], (LEVELS, LEVEL_RANK), 1.0, 4.0, (), jnp.float32),
    }


highest = lax.Precision.HIGHEST

def inner_gram(image_rows):
    return lax.dot_general(image_rows.astype(jnp.float32), image_rows.astype(jnp.float32), (((0,), (0,)), ((), ())), precision=highest, preferred_element_type=jnp.float32)

def solve_right(lower_factor, image_rows):
    return lax.linalg.triangular_solve(lower_factor, image_rows, left_side=False, lower=True, transpose_a=True)

def refine(gram_matrix, previous, row_count):
    image_rows = jnp.dot(gram_matrix.astype(jnp.float32), previous.astype(jnp.float32), precision=highest, preferred_element_type=jnp.float32)
    lower_factor = jnp.linalg.cholesky(inner_gram(image_rows) / row_count)
    return solve_right(lower_factor, image_rows)

def factor_grams(final_band_lines):
    by_level = final_band_lines.reshape(LEVELS, -1)
    level_gram = jnp.dot(by_level.astype(jnp.float32), by_level.T.astype(jnp.float32), preferred_element_type=jnp.float32)
    by_member = final_band_lines.reshape(LEVELS, MEMBERS, -1).transpose(1, 0, 2).reshape(MEMBERS, -1)
    member_gram = jnp.dot(by_member.astype(jnp.float32), by_member.T.astype(jnp.float32), preferred_element_type=jnp.float32)
    return (member_gram, level_gram)

def reference(outlook_array, earlier_location_basis, earlier_ensemble_basis, earlier_height_basis):
    location_basis_matrix = earlier_location_basis
    factor = None
    for pass_index in range(PASSES):
        reduced_tensor = jnp.dot(outlook_array.astype(jnp.float32), location_basis_matrix.astype(jnp.float32), preferred_element_type=jnp.float32).astype(jnp.bfloat16)
        ensemble_variance = lax.dot_general(outlook_array.astype(jnp.float32), reduced_tensor.astype(jnp.float32), (((0,), (0,)), ((), ())), preferred_element_type=jnp.float32)
        gram_total = inner_gram(ensemble_variance) / GRID
        factor = solve_right(jnp.linalg.cholesky(gram_total), ensemble_variance)
        location_basis_matrix = factor.astype(jnp.bfloat16)
    final_band_lines = jnp.dot(outlook_array.astype(jnp.float32), location_basis_matrix.astype(jnp.float32), preferred_element_type=jnp.float32).astype(jnp.bfloat16)
    member_gram, level_gram = factor_grams(final_band_lines)
    return (factor, refine(member_gram, earlier_ensemble_basis, MEMBERS), refine(level_gram, earlier_height_basis, LEVELS))
```

```python
import functools

import jax
import jax.numpy as jnp
from jax import lax
from jax.experimental import pallas as pl
from jax.experimental.pallas import tpu as pltpu
from jax.sharding import PartitionSpec as P

MEMBERS = 48
LEVELS = 32
PASSES = 3
RANK = 256
ROWS = 1536
GRID = 49152
EXACT = lax.Precision.HIGHEST

BLOCK = 256
BLOCKS = 7
PACKED = 28 * 2 * BLOCK
HALF = PACKED // 2
RING1 = HALF // 4
RING2 = RING1 // 4
LEAF = RING2 // 8
CHIP_COLS = 384
SHARD_ROWS = 192


def nt(a, b, precision=None):
    return lax.dot_general(
        a, b, (((1,), (1,)), ((), ())), precision=precision, preferred_element_type=jnp.float32
    )


def tn(a, b, precision=None):
    return lax.dot_general(
        a, b, (((0,), (0,)), ((), ())), precision=precision, preferred_element_type=jnp.float32
    )


def nn(a, b, precision=None):
    return jnp.dot(a, b, precision=precision, preferred_element_type=jnp.float32)


def exchange_kernel(
    x_ref, b_ref, out, xg, acc, aug, r1h, r1f, a2, r2h, r2f, a3, zbuf, send, recv
):
    s = lax.axis_index("space")
    e = lax.axis_index("ens")
    x, zh, y = s // 8, (s // 4) % 2, s % 4
    zl, c = e // 2, e % 2
    z = zh * 4 + zl
    st1, st2 = 8 - 7 * c, 1 + 7 * c
    p1 = x * (1 - c) + y * c
    p2 = y * (1 - c) + x * c

    def device(space, ens):
        return {"space": space, "ens": ens}

    partner = device(s, zl * 2 + 1 - c)

    def ring(p, st):
        right, left = (p + 1) % 4, (p + 3) % 4
        return (
            device(s + (right - p) * st, e),
            device(s + (left - p) * st, e),
            right,
            left,
            (p + 2) % 4,
        )

    ring1, ring2 = ring(p1, st1), ring(p2, st2)
    zpeers = []
    for k in range(1, 8):
        other = (z + k) % 8
        zpeers.append((device(x * 8 + (other // 4) * 4 + y, (other % 4) * 2 + c), other))

    barrier = pltpu.get_barrier_semaphore()
    greeted = [partner, ring1[0], ring1[1], ring2[0], ring2[1]] + [d for d, _ in zpeers]
    for d in greeted:
        pl.semaphore_signal(barrier, inc=1, device_id=d, device_id_type=pl.DeviceIdType.MESH)
    pl.semaphore_wait(barrier, len(greeted))

    used = [0]
    pending = []

    def start(src, dst, dev):
        n = used[0]
        used[0] += 1
        copy = pltpu.make_async_remote_copy(
            src_ref=src,
            dst_ref=dst,
            send_sem=send.at[n],
            recv_sem=recv.at[n],
            device_id=dev,
            device_id_type=pl.DeviceIdType.MESH,
        )
        copy.start()
        pending.append(copy)
        return copy

    def rows(first, count):
        return pl.ds(pl.multiple_of(first, 8), count)

    def slab_rows(chip, core):
        return pl.ds(pl.multiple_of((chip * 2 + core) * SHARD_ROWS, 64), SHARD_ROWS)

    def chip_cols(chip):
        return pl.ds(pl.multiple_of(chip * CHIP_COLS, 128), CHIP_COLS)

    mine = slab_rows(zl, c)
    moved = []
    for k in range(1, 4):
        to = (zl + k) % 4
        moved.append(start(x_ref.at[:, chip_cols(to)], xg.at[mine, :], device(s, to * 2 + c)))
    xg[mine, :] = x_ref[:, chip_cols(zl)]
    shared = [start(xg.at[mine, :], xg.at[mine, :], partner)]
    part = b_ref[pl.ds(pl.multiple_of(zl * CHIP_COLS, 128), CHIP_COLS), :]
    aug[pl.ds(ROWS, BLOCK), :] = part.astype(jnp.float32).T.astype(jnp.bfloat16)
    for k in range(1, 4):
        moved[k - 1].wait_recv()
        got = slab_rows((zl + 4 - k) % 4, c)
        shared.append(start(xg.at[got, :], xg.at[got, :], partner))
    for copy in shared:
        copy.wait_recv()
    aug[pl.ds(0, ROWS), :] = xg[...]

    @pl.loop(0, 14)
    def _(k):
        t = c * 14 + k
        i = t % BLOCKS
        j = (i + t // BLOCKS) % BLOCKS
        a = aug[pl.ds(pl.multiple_of(i * BLOCK, BLOCK), BLOCK), :]
        b = aug[pl.ds(pl.multiple_of(j * BLOCK, BLOCK), BLOCK), :]
        product = nt(a, b)
        acc[pl.ds(pl.multiple_of(k * 512, 512), 256), :] = product[:, :128]
        acc[pl.ds(pl.multiple_of(k * 512 + 256, 256), 256), :] = product[:, 128:]

    def reduce_ring(a, half_in, full_in, place, p, piece, result):
        to_right, to_left, right, left, opp = place
        h = piece // 2
        c1 = start(a.at[rows(opp * piece, h), :], half_in.at[0], to_right)
        c3 = start(a.at[rows(opp * piece + h, h), :], half_in.at[1], to_left)
        c2 = start(a.at[rows(right * piece + h, h), :], full_in.at[0, pl.ds(h, h), :], to_right)
        c4 = start(a.at[rows(left * piece, h), :], full_in.at[1, pl.ds(0, h), :], to_left)
        c1.wait_recv()
        a[rows(right * piece, h), :] = a[rows(right * piece, h), :] + half_in[0]
        c5 = start(a.at[rows(right * piece, h), :], full_in.at[0, pl.ds(0, h), :], to_right)
        c3.wait_recv()
        a[rows(left * piece + h, h), :] = a[rows(left * piece + h, h), :] + half_in[1]
        c6 = start(a.at[rows(left * piece + h, h), :], full_in.at[1, pl.ds(h, h), :], to_left)
        for copy in (c2, c4, c5, c6):
            copy.wait_recv()
        result[...] = a[rows(p * piece, piece), :] + full_in[0] + full_in[1]

    reduce_ring(acc, r1h, r1f, ring1, p1, RING1, a2)
    reduce_ring(a2, r2h, r2f, ring2, p2, RING2, a3)
    copies = [
        start(a3.at[rows(other * LEAF, LEAF), :], zbuf.at[k], d)
        for k, (d, other) in enumerate(zpeers)
    ]
    total = a3[rows(z * LEAF, LEAF), :]
    for k, copy in enumerate(copies):
        copy.wait_recv()
        total = total + zbuf[k]

    base1 = c * HALF
    base2 = base1 + p1 * RING1
    base3 = base2 + p2 * RING2
    leaf = rows(base3 + z * LEAF, LEAF)
    out[leaf, :] = total
    copies = [start(out.at[leaf, :], out.at[leaf, :], d) for d, _ in zpeers]
    for copy in copies:
        copy.wait_recv()

    def gather_ring(base, place, p, piece, on_piece):
        to_right, to_left, right, left, _ = place
        h = piece // 2

        def part(q, half):
            return rows(base + q * piece + half * h, h)

        def put(q, half, dev):
            return start(out.at[part(q, half), :], out.at[part(q, half), :], dev)

        r1 = put(p, 0, to_right)
        l1 = put(p, 1, to_left)
        r2 = put(p, 1, to_right)
        l2 = put(p, 0, to_left)
        on_piece(rows(base + p * piece, piece))
        r1.wait_recv()
        r3 = put(left, 0, to_right)
        on_piece(part(left, 0))
        l1.wait_recv()
        l3 = put(right, 1, to_left)
        on_piece(part(right, 1))
        r2.wait_recv()
        on_piece(part(left, 1))
        l2.wait_recv()
        on_piece(part(right, 0))
        r3.wait_recv()
        opp = (p + 2) % 4
        on_piece(part(opp, 0))
        l3.wait_recv()
        on_piece(part(opp, 1))

    gather_ring(base2, ring2, p2, RING2, lambda where: None)
    across = []
    gather_ring(
        base1,
        ring1,
        p1,
        RING1,
        lambda where: across.append(start(out.at[where, :], out.at[where, :], partner)),
    )
    for copy in across:
        copy.wait_recv()
    for copy in pending:
        copy.wait_send()


def exchange(outlook, basis):
    f32, bf16 = jnp.float32, jnp.bfloat16
    vmem = pl.BlockSpec(memory_space=pltpu.VMEM)
    copies = 64
    return pl.pallas_call(
        exchange_kernel,
        out_shape=(
            jax.ShapeDtypeStruct((PACKED, 128), f32),
            jax.ShapeDtypeStruct((ROWS, CHIP_COLS), bf16),
        ),
        in_specs=[vmem, vmem],
        out_specs=(vmem, vmem),
        scratch_shapes=[
            pltpu.VMEM((HALF, 128), f32),
            pltpu.VMEM((BLOCKS * BLOCK, CHIP_COLS), bf16),
            pltpu.VMEM((2, RING1 // 2, 128), f32),
            pltpu.VMEM((2, RING1, 128), f32),
            pltpu.VMEM((RING1, 128), f32),
            pltpu.VMEM((2, RING2 // 2, 128), f32),
            pltpu.VMEM((2, RING2, 128), f32),
            pltpu.VMEM((RING2, 128), f32),
            pltpu.VMEM((7, LEAF, 128), f32),
            pltpu.SemaphoreType.DMA((copies,)),
            pltpu.SemaphoreType.DMA((copies,)),
        ],
        compiler_params=pltpu.CompilerParams(
            collective_id=0, has_side_effects=True, vmem_limit_bytes=60 << 20
        ),
        name="moments",
    )(outlook, basis)


def factor_inverse(a, n):
    lanes = 2 * n
    row_id = lax.broadcasted_iota(jnp.int32, (8, lanes), 0)
    unit = (
        lax.broadcasted_iota(jnp.int32, (n, n), 0) == lax.broadcasted_iota(jnp.int32, (n, n), 1)
    ).astype(jnp.float32)
    both = jnp.concatenate([a, unit], axis=1)
    strips = [both[8 * g : 8 * g + 8, :] for g in range(n // 8)]
    scales = [jnp.zeros((8, lanes), jnp.float32) for _ in strips]
    for k in range(n):
        g0, r = divmod(k, 8)
        row = strips[g0][r : r + 1, :]
        pivot = row[:, k : k + 1]
        scales[g0] = jnp.where(row_id == r, lax.rsqrt(pivot), scales[g0])
        step = row * (1.0 / pivot)
        for g in range(g0, n // 8):
            column = strips[g][:, k : k + 1]
            if g == g0:
                column = jnp.where(row_id[:, :1] > r, column, 0.0)
            strips[g] = strips[g] - column * step
    out = jnp.concatenate([v * w for v, w in zip(strips, scales)], axis=0)
    return out[:, n:]


def factor_kernel(packed, xg, factor_ref, final_ref, khi, klo, basis, q, work, spread):
    core = lax.axis_index("ens") % 2
    for t in range(28):
        i = t % BLOCKS
        j = (i + t // BLOCKS) % BLOCKS
        if i == j == BLOCKS - 1:
            continue
        block = jnp.concatenate(
            [packed[pl.ds(t * 512, 256), :], packed[pl.ds(t * 512 + 256, 256), :]], axis=1
        )
        if i == BLOCKS - 1:
            basis[pl.ds(j * BLOCK, BLOCK), :] = block.T.astype(jnp.bfloat16)
            continue
        hi = block.astype(jnp.bfloat16)
        if j == BLOCKS - 1:
            basis[pl.ds(i * BLOCK, BLOCK), :] = hi
            continue
        lo = (block - hi.astype(jnp.float32)).astype(jnp.bfloat16)
        at_i, at_j = pl.ds(i * BLOCK, BLOCK), pl.ds(j * BLOCK, BLOCK)
        khi[at_i, at_j] = hi
        klo[at_i, at_j] = lo
        if i != j:
            khi[at_j, at_i] = hi.astype(jnp.float32).T.astype(jnp.bfloat16)
            klo[at_j, at_i] = lo.astype(jnp.float32).T.astype(jnp.bfloat16)

    unit = (
        lax.broadcasted_iota(jnp.int32, (RANK, RANK), 0)
        == lax.broadcasted_iota(jnp.int32, (RANK, RANK), 1)
    ).astype(jnp.float32)

    def one_pass(index, carry):
        work[:, pl.ds(0, RANK)] = jnp.zeros((RANK, RANK), jnp.float32)
        work[:, pl.ds(RANK, RANK)] = unit

        @pl.loop(0, 6)
        def _(i):
            at = pl.ds(pl.multiple_of(i * BLOCK, BLOCK), BLOCK)
            image = nn(khi[at, :], basis[...]) + nn(klo[at, :], basis[...])
            q[at, :] = image
            work[:, pl.ds(0, RANK)] += tn(basis[at, :].astype(jnp.float32), image, EXACT)

        work[:, pl.ds(0, RANK)] = work[:, pl.ds(0, RANK)] * (1.0 / GRID)
        for p in range(4):
            top = 64 * p
            inverse = factor_inverse(work[pl.ds(top, 64), pl.ds(top, 64)], 64)
            panel = nn(inverse, work[pl.ds(top, 64), :], EXACT)
            work[pl.ds(top, 64), :] = panel
            if p < 3:
                rest = 256 - top - 64
                work[pl.ds(top + 64, rest), :] -= tn(panel[:, top + 64 : 256], panel, EXACT)
        solve = work[:, pl.ds(RANK, RANK)]

        @pl.when(index == PASSES - 1)
        def _():
            spread[...] = tn(xg[...], basis[...])
            own = spread[pl.ds(pl.multiple_of(core * SHARD_ROWS, 64), SHARD_ROWS), :]
            factor_ref[...] = nt(own, solve, EXACT)

        @pl.loop(0, 6)
        def _(i):
            at = pl.ds(pl.multiple_of(i * BLOCK, BLOCK), BLOCK)
            basis[at, :] = nt(q[at, :], solve, EXACT).astype(jnp.bfloat16)

        return carry

    lax.fori_loop(0, PASSES, one_pass, 0)
    final_ref[...] = basis[...]


def factors(packed, xg):
    f32, bf16 = jnp.float32, jnp.bfloat16
    vmem = pl.BlockSpec(memory_space=pltpu.VMEM)
    return pl.pallas_call(
        factor_kernel,
        out_shape=(
            jax.ShapeDtypeStruct((SHARD_ROWS, RANK), f32),
            jax.ShapeDtypeStruct((ROWS, RANK), bf16),
        ),
        in_specs=[vmem, vmem],
        out_specs=(vmem, vmem),
        scratch_shapes=[
            pltpu.VMEM((ROWS, ROWS), bf16),
            pltpu.VMEM((ROWS, ROWS), bf16),
            pltpu.VMEM((ROWS, RANK), bf16),
            pltpu.VMEM((ROWS, RANK), f32),
            pltpu.VMEM((RANK, 2 * RANK), f32),
            pltpu.VMEM((CHIP_COLS, RANK), f32),
        ],
        compiler_params=pltpu.CompilerParams(vmem_limit_bytes=60 << 20),
        name="passes",
    )(packed, xg)


def inner_gram(image_rows):
    return tn(image_rows, image_rows, EXACT)


def solve_right(lower_factor, image_rows):
    return lax.linalg.triangular_solve(
        lower_factor, image_rows, left_side=False, lower=True, transpose_a=True
    )


def refine(gram_matrix, previous, row_count):
    image_rows = nn(gram_matrix, previous, EXACT)
    lower_factor = jnp.linalg.cholesky(inner_gram(image_rows) / row_count)
    return solve_right(lower_factor, image_rows)


def factor_grams(final_band_lines):
    by_level = final_band_lines.reshape(LEVELS, -1)
    level_gram = jnp.dot(by_level, by_level.T, preferred_element_type=jnp.float32)
    by_member = (
        final_band_lines.reshape(LEVELS, MEMBERS, -1).transpose(1, 0, 2).reshape(MEMBERS, -1)
    )
    member_gram = jnp.dot(by_member, by_member.T, preferred_element_type=jnp.float32)
    return (member_gram, level_gram)


def on_device(outlook_array, earlier_location_basis, earlier_ensemble_basis, earlier_height_basis):
    packed, slab = exchange(outlook_array, earlier_location_basis)
    factor, final = factors(packed, slab)
    member_gram, level_gram = factor_grams(final)
    return (
        factor,
        refine(member_gram, earlier_ensemble_basis, MEMBERS),
        refine(level_gram, earlier_height_basis, LEVELS),
    )


def solution(mesh):
    in_specs = (P("ens", "space"), P("space", None), P(), P())
    out_specs = (P(("space", "ens"), None), P(), P())
    return jax.shard_map(
        on_device, mesh=mesh, in_specs=in_specs, out_specs=out_specs, check_vma=False
    )
```

```python
import functools

import jax
import jax.numpy as jnp
from jax import lax
from jax.experimental import pallas as pl
from jax.experimental.pallas import tpu as pltpu
from jax.sharding import PartitionSpec as P

MEMBERS = 48
LEVELS = 32
PASSES = 3
RANK = 256
ROWS = 1536
GRID = 49152
EXACT = lax.Precision.HIGHEST

BLOCK = 256
BLOCKS = 7
PACKED = 28 * 2 * BLOCK
HALF = PACKED // 2
RING1 = HALF // 4
RING2 = RING1 // 4
LEAF = RING2 // 8
CHIP_COLS = 384
SHARD_ROWS = 192


def nt(a, b, precision=None):
    return lax.dot_general(
        a, b, (((1,), (1,)), ((), ())), precision=precision, preferred_element_type=jnp.float32
    )


def tn(a, b, precision=None):
    return lax.dot_general(
        a, b, (((0,), (0,)), ((), ())), precision=precision, preferred_element_type=jnp.float32
    )


def nn(a, b, precision=None):
    return jnp.dot(a, b, precision=precision, preferred_element_type=jnp.float32)


def exchange_kernel(
    x_ref, b_ref, out, xg, acc, aug, r1h, r1f, a2, r2h, r2f, a3, zbuf, send, recv
):
    s = lax.axis_index("space")
    e = lax.axis_index("ens")
    x, zh, y = s // 8, (s // 4) % 2, s % 4
    zl, c = e // 2, e % 2
    z = zh * 4 + zl
    st1, st2 = 8 - 7 * c, 1 + 7 * c
    p1 = x * (1 - c) + y * c
    p2 = y * (1 - c) + x * c

    def device(space, ens):
        return {"space": space, "ens": ens}

    partner = device(s, zl * 2 + 1 - c)

    def ring(p, st):
        right, left = (p + 1) % 4, (p + 3) % 4
        return (
            device(s + (right - p) * st, e),
            device(s + (left - p) * st, e),
            right,
            left,
            (p + 2) % 4,
        )

    ring1, ring2 = ring(p1, st1), ring(p2, st2)
    zpeers = []
    for k in range(1, 8):
        other = (z + k) % 8
        zpeers.append((device(x * 8 + (other // 4) * 4 + y, (other % 4) * 2 + c), other))

    barrier = pltpu.get_barrier_semaphore()
    greeted = [partner, ring1[0], ring1[1], ring2[0], ring2[1]] + [d for d, _ in zpeers]
    for d in greeted:
        pl.semaphore_signal(barrier, inc=1, device_id=d, device_id_type=pl.DeviceIdType.MESH)
    pl.semaphore_wait(barrier, len(greeted))

    used = [0]
    pending = []

    def start(src, dst, dev):
        n = used[0]
        used[0] += 1
        copy = pltpu.make_async_remote_copy(
            src_ref=src,
            dst_ref=dst,
            send_sem=send.at[n],
            recv_sem=recv.at[n],
            device_id=dev,
            device_id_type=pl.DeviceIdType.MESH,
        )
        copy.start()
        pending.append(copy)
        return copy

    def rows(first, count):
        return pl.ds(pl.multiple_of(first, 8), count)

    def slab_rows(chip, core):
        return pl.ds(pl.multiple_of((chip * 2 + core) * SHARD_ROWS, 64), SHARD_ROWS)

    def chip_cols(chip):
        return pl.ds(pl.multiple_of(chip * CHIP_COLS, 128), CHIP_COLS)

    mine = slab_rows(zl, c)
    moved = []
    for k in range(1, 4):
        to = (zl + k) % 4
        moved.append(start(x_ref.at[:, chip_cols(to)], xg.at[mine, :], device(s, to * 2 + c)))
    xg[mine, :] = x_ref[:, chip_cols(zl)]
    shared = [start(xg.at[mine, :], xg.at[mine, :], partner)]
    part = b_ref[pl.ds(pl.multiple_of(zl * CHIP_COLS, 128), CHIP_COLS), :]
    aug[pl.ds(ROWS, BLOCK), :] = part.astype(jnp.float32).T.astype(jnp.bfloat16)
    for k in range(1, 4):
        moved[k - 1].wait_recv()
        got = slab_rows((zl + 4 - k) % 4, c)
        shared.append(start(xg.at[got, :], xg.at[got, :], partner))
    for copy in shared:
        copy.wait_recv()
    aug[pl.ds(0, ROWS), :] = xg[...]

    @pl.loop(0, 14)
    def _(k):
        t = c * 14 + k
        i = t % BLOCKS
        j = (i + t // BLOCKS) % BLOCKS
        a = aug[pl.ds(pl.multiple_of(i * BLOCK, BLOCK), BLOCK), :]
        b = aug[pl.ds(pl.multiple_of(j * BLOCK, BLOCK), BLOCK), :]
        product = nt(a, b)
        acc[pl.ds(pl.multiple_of(k * 512, 512), 256), :] = product[:, :128]
        acc[pl.ds(pl.multiple_of(k * 512 + 256, 256), 256), :] = product[:, 128:]

    def reduce_ring(a, half_in, full_in, place, p, piece, result):
        to_right, to_left, right, left, opp = place
        h = piece // 2
        c1 = start(a.at[rows(opp * piece, h), :], half_in.at[0], to_right)
        c3 = start(a.at[rows(opp * piece + h, h), :], half_in.at[1], to_left)
        c2 = start(a.at[rows(right * piece + h, h), :], full_in.at[0, pl.ds(h, h), :], to_right)
        c4 = start(a.at[rows(left * piece, h), :], full_in.at[1, pl.ds(0, h), :], to_left)
        c1.wait_recv()
        a[rows(right * piece, h), :] = a[rows(right * piece, h), :] + half_in[0]
        c5 = start(a.at[rows(right * piece, h), :], full_in.at[0, pl.ds(0, h), :], to_right)
        c3.wait_recv()
        a[rows(left * piece + h, h), :] = a[rows(left * piece + h, h), :] + half_in[1]
        c6 = start(a.at[rows(left * piece + h, h), :], full_in.at[1, pl.ds(h, h), :], to_left)
        for copy in (c2, c4, c5, c6):
            copy.wait_recv()
        result[...] = a[rows(p * piece, piece), :] + full_in[0] + full_in[1]

    reduce_ring(acc, r1h, r1f, ring1, p1, RING1, a2)
    reduce_ring(a2, r2h, r2f, ring2, p2, RING2, a3)
    copies = [
        start(a3.at[rows(other * LEAF, LEAF), :], zbuf.at[k], d)
        for k, (d, other) in enumerate(zpeers)
    ]
    total = a3[rows(z * LEAF, LEAF), :]
    for k, copy in enumerate(copies):
        copy.wait_recv()
        total = total + zbuf[k]

    base1 = c * HALF
    base2 = base1 + p1 * RING1
    base3 = base2 + p2 * RING2
    leaf = rows(base3 + z * LEAF, LEAF)
    out[leaf, :] = total
    copies = [start(out.at[leaf, :], out.at[leaf, :], d) for d, _ in zpeers]
    for copy in copies:
        copy.wait_recv()

    def gather_ring(base, place, p, piece, on_piece):
        to_right, to_left, right, left, _ = place
        h = piece // 2

        def part(q, half):
            return rows(base + q * piece + half * h, h)

        def put(q, half, dev):
            return start(out.at[part(q, half), :], out.at[part(q, half), :], dev)

        r1 = put(p, 0, to_right)
        l1 = put(p, 1, to_left)
        r2 = put(p, 1, to_right)
        l2 = put(p, 0, to_left)
        on_piece(rows(base + p * piece, piece))
        r1.wait_recv()
        r3 = put(left, 0, to_right)
        on_piece(part(left, 0))
        l1.wait_recv()
        l3 = put(right, 1, to_left)
        on_piece(part(right, 1))
        r2.wait_recv()
        on_piece(part(left, 1))
        l2.wait_recv()
        on_piece(part(right, 0))
        r3.wait_recv()
        opp = (p + 2) % 4
        on_piece(part(opp, 0))
        l3.wait_recv()
        on_piece(part(opp, 1))

    gather_ring(base2, ring2, p2, RING2, lambda where: None)
    across = []
    gather_ring(
        base1,
        ring1,
        p1,
        RING1,
        lambda where: across.append(start(out.at[where, :], out.at[where, :], partner)),
    )
    for copy in across:
        copy.wait_recv()
    for copy in pending:
        copy.wait_send()


def exchange(outlook, basis):
    f32, bf16 = jnp.float32, jnp.bfloat16
    vmem = pl.BlockSpec(memory_space=pltpu.VMEM)
    copies = 64
    return pl.pallas_call(
        exchange_kernel,
        out_shape=(
            jax.ShapeDtypeStruct((PACKED, 128), f32),
            jax.ShapeDtypeStruct((ROWS, CHIP_COLS), bf16),
        ),
        in_specs=[vmem, vmem],
        out_specs=(vmem, vmem),
        scratch_shapes=[
            pltpu.VMEM((HALF, 128), f32),
            pltpu.VMEM((BLOCKS * BLOCK, CHIP_COLS), bf16),
            pltpu.VMEM((2, RING1 // 2, 128), f32),
            pltpu.VMEM((2, RING1, 128), f32),
            pltpu.VMEM((RING1, 128), f32),
            pltpu.VMEM((2, RING2 // 2, 128), f32),
            pltpu.VMEM((2, RING2, 128), f32),
            pltpu.VMEM((RING2, 128), f32),
            pltpu.VMEM((7, LEAF, 128), f32),
            pltpu.SemaphoreType.DMA((copies,)),
            pltpu.SemaphoreType.DMA((copies,)),
        ],
        compiler_params=pltpu.CompilerParams(
            collective_id=0, has_side_effects=True, vmem_limit_bytes=60 << 20
        ),
        name="moments",
    )(outlook, basis)


def split(a):
    first = a.astype(jnp.bfloat16)
    rest = a - first.astype(jnp.float32)
    second = rest.astype(jnp.bfloat16)
    return first, second, (rest - second.astype(jnp.float32)).astype(jnp.bfloat16)


def factor_inverse(a, n):
    lanes = 2 * n
    full = (8, lanes)
    row_id = lax.broadcasted_iota(jnp.int32, full, 0)
    unit = (
        lax.broadcasted_iota(jnp.int32, (n, n), 0) == lax.broadcasted_iota(jnp.int32, (n, n), 1)
    ).astype(jnp.float32)
    both = jnp.concatenate([a, unit], axis=1)
    count = n // 8
    strips = [both[8 * g : 8 * g + 8, :] for g in range(count)]
    for own in range(count):
        columns = {
            g: [
                jnp.broadcast_to(strips[g][:, 8 * own + m : 8 * own + m + 1], full)
                for m in range(8)
            ]
            for g in range(own, count)
        }
        lines = [jnp.broadcast_to(strips[own][r : r + 1, :], full) for r in range(8)]
        corner = {
            (r, m): jnp.broadcast_to(columns[own][m][r : r + 1, :], full)
            for r in range(8)
            for m in range(r, 8)
        }
        ratio, inverse, scale = {}, [], []
        for r in range(8):
            pivot = corner[r, r]
            inverse.append(1.0 / pivot)
            scale.append(lax.rsqrt(pivot))
            for m in range(r + 1, 8):
                ratio[r, m] = corner[r, m] * inverse[r]
            for low in range(r + 1, 8):
                for m in range(low, 8):
                    corner[low, m] = corner[low, m] - corner[r, low] * ratio[r, m]
        for r in range(8):
            for m in range(r + 1, 8):
                lines[m] = lines[m] - ratio[r, m] * lines[r]
        for g in range(own + 1, count):
            column = columns[g]
            for r in range(8):
                for m in range(r + 1, 8):
                    column[m] = column[m] - column[r] * ratio[r, m]
            for r in range(8):
                strips[g] = strips[g] - (column[r] * inverse[r]) * lines[r]
        done = lines[0] * scale[0]
        for r in range(1, 8):
            done = jnp.where(row_id == r, lines[r] * scale[r], done)
        strips[own] = done
    return jnp.concatenate(strips, axis=0)[:, n:]


def factor_kernel(packed, xg, factor_ref, final_ref, khi, klo, basis, q, work, spread):
    core = lax.axis_index("ens") % 2
    for t in range(28):
        i = t % BLOCKS
        j = (i + t // BLOCKS) % BLOCKS
        if i == j == BLOCKS - 1:
            continue
        block = jnp.concatenate(
            [packed[pl.ds(t * 512, 256), :], packed[pl.ds(t * 512 + 256, 256), :]], axis=1
        )
        if i == BLOCKS - 1:
            basis[pl.ds(j * BLOCK, BLOCK), :] = block.T.astype(jnp.bfloat16)
            continue
        hi = block.astype(jnp.bfloat16)
        if j == BLOCKS - 1:
            basis[pl.ds(i * BLOCK, BLOCK), :] = hi
            continue
        lo = (block - hi.astype(jnp.float32)).astype(jnp.bfloat16)
        at_i, at_j = pl.ds(i * BLOCK, BLOCK), pl.ds(j * BLOCK, BLOCK)
        khi[at_i, at_j] = hi
        klo[at_i, at_j] = lo
        if i != j:
            khi[at_j, at_i] = hi.astype(jnp.float32).T.astype(jnp.bfloat16)
            klo[at_j, at_i] = lo.astype(jnp.float32).T.astype(jnp.bfloat16)

    unit = (
        lax.broadcasted_iota(jnp.int32, (RANK, RANK), 0)
        == lax.broadcasted_iota(jnp.int32, (RANK, RANK), 1)
    ).astype(jnp.float32)

    def one_pass(index, carry):
        work[:, pl.ds(0, RANK)] = jnp.zeros((RANK, RANK), jnp.float32)
        work[:, pl.ds(RANK, RANK)] = unit

        for i in range(6):
            at = pl.ds(i * BLOCK, BLOCK)
            image = nn(khi[at, :], basis[...]) + nn(klo[at, :], basis[...])
            q[at, :] = image
            parts = split(image)
            line = basis[at, :].astype(jnp.float32).T.astype(jnp.bfloat16)
            work[:, pl.ds(0, RANK)] += (nn(line, parts[0]) + nn(line, parts[1])) + nn(line, parts[2])

        work[:, pl.ds(0, RANK)] = work[:, pl.ds(0, RANK)] * (1.0 / GRID)
        for p in range(4):
            top = 64 * p
            inverse = factor_inverse(work[pl.ds(top, 64), pl.ds(top, 64)], 64)
            panel = nn(inverse, work[pl.ds(top, 64), :], EXACT)
            work[pl.ds(top, 64), :] = panel
            if p < 3:
                rest = 256 - top - 64
                work[pl.ds(top + 64, rest), :] -= tn(panel[:, top + 64 : 256], panel, EXACT)
        solve = work[:, pl.ds(RANK, RANK)]

        @pl.when(index == PASSES - 1)
        def _():
            spread[...] = tn(xg[...], basis[...])
            own = spread[pl.ds(pl.multiple_of(core * SHARD_ROWS, 64), SHARD_ROWS), :]
            factor_ref[...] = nt(own, solve, EXACT)

        @pl.loop(0, 6)
        def _(i):
            at = pl.ds(pl.multiple_of(i * BLOCK, BLOCK), BLOCK)
            basis[at, :] = nt(q[at, :], solve, EXACT).astype(jnp.bfloat16)

        return carry

    lax.fori_loop(0, PASSES, one_pass, 0)
    final_ref[...] = basis[...]


def factors(packed, xg):
    f32, bf16 = jnp.float32, jnp.bfloat16
    vmem = pl.BlockSpec(memory_space=pltpu.VMEM)
    return pl.pallas_call(
        factor_kernel,
        out_shape=(
            jax.ShapeDtypeStruct((SHARD_ROWS, RANK), f32),
            jax.ShapeDtypeStruct((ROWS, RANK), bf16),
        ),
        in_specs=[vmem, vmem],
        out_specs=(vmem, vmem),
        scratch_shapes=[
            pltpu.VMEM((ROWS, ROWS), bf16),
            pltpu.VMEM((ROWS, ROWS), bf16),
            pltpu.VMEM((ROWS, RANK), bf16),
            pltpu.VMEM((ROWS, RANK), f32),
            pltpu.VMEM((RANK, 2 * RANK), f32),
            pltpu.VMEM((CHIP_COLS, RANK), f32),
        ],
        compiler_params=pltpu.CompilerParams(vmem_limit_bytes=60 << 20),
        name="passes",
    )(packed, xg)


def inner_gram(image_rows):
    return tn(image_rows, image_rows, EXACT)


def solve_right(lower_factor, image_rows):
    return lax.linalg.triangular_solve(
        lower_factor, image_rows, left_side=False, lower=True, transpose_a=True
    )


def refine(gram_matrix, previous, row_count):
    image_rows = nn(gram_matrix, previous, EXACT)
    lower_factor = jnp.linalg.cholesky(inner_gram(image_rows) / row_count)
    return solve_right(lower_factor, image_rows)


def factor_grams(final_band_lines):
    by_level = final_band_lines.reshape(LEVELS, -1)
    level_gram = jnp.dot(by_level, by_level.T, preferred_element_type=jnp.float32)
    by_member = (
        final_band_lines.reshape(LEVELS, MEMBERS, -1).transpose(1, 0, 2).reshape(MEMBERS, -1)
    )
    member_gram = jnp.dot(by_member, by_member.T, preferred_element_type=jnp.float32)
    return (member_gram, level_gram)


def on_device(outlook_array, earlier_location_basis, earlier_ensemble_basis, earlier_height_basis):
    packed, slab = exchange(outlook_array, earlier_location_basis)
    factor, final = factors(packed, slab)
    member_gram, level_gram = factor_grams(final)
    return (
        factor,
        refine(member_gram, earlier_ensemble_basis, MEMBERS),
        refine(level_gram, earlier_height_basis, LEVELS),
    )


def solution(mesh):
    in_specs = (P("ens", "space"), P("space", None), P(), P())
    out_specs = (P(("space", "ens"), None), P(), P())
    return jax.shard_map(
        on_device, mesh=mesh, in_specs=in_specs, out_specs=out_specs, check_vma=False
    )
```

```python
import functools

import jax
import jax.numpy as jnp
from jax import lax
from jax.experimental import pallas as pl
from jax.experimental.pallas import tpu as pltpu
from jax.sharding import PartitionSpec as P

MEMBERS = 48
LEVELS = 32
PASSES = 3
RANK = 256
ROWS = 1536
GRID = 49152
EXACT = lax.Precision.HIGHEST

BLOCK = 256
BLOCKS = 7
SPAN = BLOCKS * BLOCK
HALF = 14 * 2 * BLOCK
CHIP_COLS = 384
SHARD_ROWS = 192
UNITS = (3, 2, 2)
UNIT = 1024
COPIES = 200


def nt(a, b, precision=None):
    return lax.dot_general(
        a, b, (((1,), (1,)), ((), ())), precision=precision, preferred_element_type=jnp.float32
    )


def tn(a, b, precision=None):
    return lax.dot_general(
        a, b, (((0,), (0,)), ((), ())), precision=precision, preferred_element_type=jnp.float32
    )


def nn(a, b, precision=None):
    return jnp.dot(a, b, precision=precision, preferred_element_type=jnp.float32)


def exchange_kernel(
    x_ref, b_ref, high, low, xg, out, acc, aug, r1h, r1f, a2, r2h, r2f, a3, zbuf, send, recv
):
    s = lax.axis_index("space")
    e = lax.axis_index("ens")
    x, zh, y = s // 8, (s // 4) % 2, s % 4
    zl, c = e // 2, e % 2
    z = zh * 4 + zl
    st1, st2 = 8 - 7 * c, 1 + 7 * c
    p1 = x * (1 - c) + y * c
    p2 = y * (1 - c) + x * c

    def device(space, ens):
        return {"space": space, "ens": ens}

    partner = device(s, zl * 2 + 1 - c)

    def ring(p, st):
        right, left = (p + 1) % 4, (p + 3) % 4
        return (
            device(s + (right - p) * st, e),
            device(s + (left - p) * st, e),
            right,
            left,
            (p + 2) % 4,
        )

    ring1, ring2 = ring(p1, st1), ring(p2, st2)
    zpeers = []
    for k in range(1, 8):
        other = (z + k) % 8
        zpeers.append((device(x * 8 + (other // 4) * 4 + y, (other % 4) * 2 + c), other))

    barrier = pltpu.get_barrier_semaphore()
    greeted = [partner, ring1[0], ring1[1], ring2[0], ring2[1]] + [d for d, _ in zpeers]
    for d in greeted:
        pl.semaphore_signal(barrier, inc=1, device_id=d, device_id_type=pl.DeviceIdType.MESH)
    pl.semaphore_wait(barrier, len(greeted))

    pending = []

    def start(src, dst, dev):
        n = len(pending)
        copy = pltpu.make_async_remote_copy(
            src_ref=src,
            dst_ref=dst,
            send_sem=send.at[n],
            recv_sem=recv.at[n],
            device_id=dev,
            device_id_type=pl.DeviceIdType.MESH,
        )
        copy.start()
        pending.append(copy)
        return copy

    def rows(first, count):
        return pl.ds(pl.multiple_of(first, 8), count)

    def slab_rows(chip, core):
        return pl.ds(pl.multiple_of((chip * 2 + core) * SHARD_ROWS, 64), SHARD_ROWS)

    def chip_cols(chip):
        return pl.ds(pl.multiple_of(chip * CHIP_COLS, 128), CHIP_COLS)

    mine = slab_rows(zl, c)
    moved = []
    for k in range(1, 4):
        to = (zl + k) % 4
        moved.append(start(x_ref.at[:, chip_cols(to)], xg.at[mine, :], device(s, to * 2 + c)))
    xg[mine, :] = x_ref[:, chip_cols(zl)]
    shared = [start(xg.at[mine, :], xg.at[mine, :], partner)]
    part = b_ref[pl.ds(pl.multiple_of(zl * CHIP_COLS, 128), CHIP_COLS), :]
    aug[pl.ds(ROWS, BLOCK), :] = part.astype(jnp.float32).T.astype(jnp.bfloat16)
    for k in range(1, 4):
        moved[k - 1].wait_recv()
        got = slab_rows((zl + 4 - k) % 4, c)
        shared.append(start(xg.at[got, :], xg.at[got, :], partner))
    for copy in shared:
        copy.wait_recv()
    aug[pl.ds(0, ROWS), :] = xg[...]

    def block_of(t):
        i = t % BLOCKS
        j = (i + t // BLOCKS) % BLOCKS
        return (
            pl.ds(pl.multiple_of(i * BLOCK, BLOCK), BLOCK),
            pl.ds(pl.multiple_of(j * BLOCK, BLOCK), BLOCK),
        )

    def unpack(core, first, count):
        @pl.loop(first, first + count)
        def _(k):
            at_i, at_j = block_of(core * 14 + k)
            top = pl.multiple_of(core * HALF + k * 512, 256)
            block = jnp.concatenate(
                [out[pl.ds(top, 256), :], out[pl.ds(top + 256, 256), :]], axis=1
            )
            for value, r, w in ((block, at_i, at_j), (block.T, at_j, at_i)):
                first_part = value.astype(jnp.bfloat16)
                high[r, w] = first_part
                low[r, w] = (value - first_part.astype(jnp.float32)).astype(jnp.bfloat16)

    def chain(chunk):
        units = UNITS[chunk]
        before = sum(UNITS[:chunk])
        off = before * UNIT
        clock = 1.9 * before

        @pl.loop(2 * before, 2 * (before + units))
        def _(k):
            at_i, at_j = block_of(c * 14 + k)
            product = nt(aug[at_i, :], aug[at_j, :])
            acc[pl.ds(pl.multiple_of(k * 512, 512), 256), :] = product[:, :128]
            acc[pl.ds(pl.multiple_of(k * 512 + 256, 256), 256), :] = product[:, 128:]

        def reduce_ring(a, base, half_in, full_in, place, p, piece, result, at, took):
            to_right, to_left, right, left, opp = place
            h = piece // 2
            hs = pl.ds(at // 2, h)

            def full(side, half):
                return full_in.at[side, pl.ds(at + half * h, h), :]

            def mine_at(q, half):
                return rows(base + q * piece + half * h, h)

            c1 = start(a.at[mine_at(opp, 0), :], half_in.at[0, hs, :], to_right)
            c3 = start(a.at[mine_at(opp, 1), :], half_in.at[1, hs, :], to_left)
            c2 = start(a.at[mine_at(right, 1), :], full(0, 1), to_right)
            c4 = start(a.at[mine_at(left, 0), :], full(1, 0), to_left)
            yield took / 3
            c1.wait_recv()
            a[mine_at(right, 0), :] = a[mine_at(right, 0), :] + half_in[0, hs, :]
            c5 = start(a.at[mine_at(right, 0), :], full(0, 0), to_right)
            c3.wait_recv()
            a[mine_at(left, 1), :] = a[mine_at(left, 1), :] + half_in[1, hs, :]
            c6 = start(a.at[mine_at(left, 1), :], full(1, 1), to_left)
            yield took
            for copy in (c2, c4, c5, c6):
                copy.wait_recv()
            where = pl.ds(at, piece)
            result[where, :] = (
                a[rows(base + p * piece, piece), :] + full_in[0, where, :] + full_in[1, where, :]
            )

        piece1, piece2, leaf = units * UNIT // 4, units * UNIT // 16, units * UNIT // 128
        at1, at2, at3 = off // 4, off // 16, off // 128
        for wait in reduce_ring(acc, off, r1h, r1f, ring1, p1, piece1, a2, at1, 1.9 * units + 2):
            yield clock + wait
        clock += 1.9 * units + 2
        for wait in reduce_ring(a2, at1, r2h, r2f, ring2, p2, piece2, a3, at2, 0.5 * units + 3):
            yield clock + wait
        clock += 0.5 * units + 3
        copies = [
            start(a3.at[rows(at2 + other * leaf, leaf), :], zbuf.at[k, pl.ds(at3, leaf), :], d)
            for k, (d, other) in enumerate(zpeers)
        ]
        clock += 0.7 * units + 3
        yield clock
        total = a3[rows(at2 + z * leaf, leaf), :]
        for k, copy in enumerate(copies):
            copy.wait_recv()
            total = total + zbuf[k, pl.ds(at3, leaf), :]

        base1 = c * HALF + off
        base2 = base1 + p1 * piece1
        base3 = base2 + p2 * piece2
        own = rows(base3 + z * leaf, leaf)
        out[own, :] = total
        copies = [start(out.at[own, :], out.at[own, :], d) for d, _ in zpeers]
        clock += 0.7 * units + 3
        yield clock
        for copy in copies:
            copy.wait_recv()

        def gather_ring(base, place, p, piece, took, on_piece):
            to_right, to_left, right, left, opp = place
            h = piece // 2

            def part(q, half):
                return rows(base + q * piece + half * h, h)

            def put(q, half, dev):
                return start(out.at[part(q, half), :], out.at[part(q, half), :], dev)

            r1 = put(p, 0, to_right)
            l1 = put(p, 1, to_left)
            r2 = put(p, 1, to_right)
            l2 = put(p, 0, to_left)
            on_piece(rows(base + p * piece, piece))
            yield took / 3
            r1.wait_recv()
            r3 = put(left, 0, to_right)
            on_piece(part(left, 0))
            l1.wait_recv()
            l3 = put(right, 1, to_left)
            on_piece(part(right, 1))
            yield 2 * took / 3
            r2.wait_recv()
            on_piece(part(left, 1))
            l2.wait_recv()
            on_piece(part(right, 0))
            yield took
            r3.wait_recv()
            on_piece(part(opp, 0))
            l3.wait_recv()
            on_piece(part(opp, 1))

        for wait in gather_ring(base2, ring2, p2, piece2, 0.5 * units + 3, lambda where: None):
            yield clock + wait
        clock += 0.5 * units + 3
        across = []
        for wait in gather_ring(
            base1,
            ring1,
            p1,
            piece1,
            1.9 * units + 2,
            lambda where: across.append(start(out.at[where, :], out.at[where, :], partner)),
        ):
            yield clock + wait
        clock += 1.9 * units + 2
        unpack(c, 2 * before, 2 * units)
        yield clock + 3
        for copy in across:
            copy.wait_recv()
        unpack(1 - c, 2 * before, 2 * units)

    chains = {n: chain(n) for n in range(len(UNITS))}
    due = {n: next(one) for n, one in chains.items()}
    while due:
        n = min(due, key=lambda one: due[one])
        value = next(chains[n], None)
        if value is None:
            del due[n]
        else:
            due[n] = value
    for copy in pending:
        copy.wait_send()


def exchange(outlook, basis):
    f32, bf16 = jnp.float32, jnp.bfloat16
    vmem = pl.BlockSpec(memory_space=pltpu.VMEM)
    return pl.pallas_call(
        exchange_kernel,
        out_shape=(
            jax.ShapeDtypeStruct((SPAN, SPAN), bf16),
            jax.ShapeDtypeStruct((SPAN, SPAN), bf16),
            jax.ShapeDtypeStruct((ROWS, CHIP_COLS), bf16),
        ),
        in_specs=[vmem, vmem],
        out_specs=(vmem, vmem, vmem),
        scratch_shapes=[
            pltpu.VMEM((2 * HALF, 128), f32),
            pltpu.VMEM((HALF, 128), f32),
            pltpu.VMEM((SPAN, CHIP_COLS), bf16),
            pltpu.VMEM((2, HALF // 8, 128), f32),
            pltpu.VMEM((2, HALF // 4, 128), f32),
            pltpu.VMEM((HALF // 4, 128), f32),
            pltpu.VMEM((2, HALF // 32, 128), f32),
            pltpu.VMEM((2, HALF // 16, 128), f32),
            pltpu.VMEM((HALF // 16, 128), f32),
            pltpu.VMEM((7, HALF // 128, 128), f32),
            pltpu.SemaphoreType.DMA((COPIES,)),
            pltpu.SemaphoreType.DMA((COPIES,)),
        ],
        compiler_params=pltpu.CompilerParams(
            collective_id=0, has_side_effects=True, vmem_limit_bytes=36 << 20
        ),
        name="moments",
    )(outlook, basis)


def split(a):
    first = a.astype(jnp.bfloat16)
    rest = a - first.astype(jnp.float32)
    second = rest.astype(jnp.bfloat16)
    return first, second, (rest - second.astype(jnp.float32)).astype(jnp.bfloat16)


def factor_inverse(a, n):
    lanes = 2 * n
    full = (8, lanes)
    row_id = lax.broadcasted_iota(jnp.int32, full, 0)
    unit = (
        lax.broadcasted_iota(jnp.int32, (n, n), 0) == lax.broadcasted_iota(jnp.int32, (n, n), 1)
    ).astype(jnp.float32)
    both = jnp.concatenate([a, unit], axis=1)
    count = n // 8
    strips = [both[8 * g : 8 * g + 8, :] for g in range(count)]
    for own in range(count):
        columns = {
            g: [
                jnp.broadcast_to(strips[g][:, 8 * own + m : 8 * own + m + 1], full)
                for m in range(8)
            ]
            for g in range(own, count)
        }
        lines = [jnp.broadcast_to(strips[own][r : r + 1, :], full) for r in range(8)]
        corner = {
            (r, m): jnp.broadcast_to(columns[own][m][r : r + 1, :], full)
            for r in range(8)
            for m in range(r, 8)
        }
        ratio, inverse, scale = {}, [], []
        for r in range(8):
            pivot = corner[r, r]
            inverse.append(1.0 / pivot)
            scale.append(lax.rsqrt(pivot))
            for m in range(r + 1, 8):
                ratio[r, m] = corner[r, m] * inverse[r]
            for low in range(r + 1, 8):
                for m in range(low, 8):
                    corner[low, m] = corner[low, m] - corner[r, low] * ratio[r, m]
        for r in range(8):
            for m in range(r + 1, 8):
                lines[m] = lines[m] - ratio[r, m] * lines[r]
        for g in range(own + 1, count):
            column = columns[g]
            for r in range(8):
                for m in range(r + 1, 8):
                    column[m] = column[m] - column[r] * ratio[r, m]
            for r in range(8):
                strips[g] = strips[g] - (column[r] * inverse[r]) * lines[r]
        done = lines[0] * scale[0]
        for r in range(1, 8):
            done = jnp.where(row_id == r, lines[r] * scale[r], done)
        strips[own] = done
    return jnp.concatenate(strips, axis=0)[:, n:]


def factor_kernel(high, low, xg, factor_ref, final_ref, basis, q, work, spread):
    core = lax.axis_index("ens") % 2
    basis[...] = high[pl.ds(0, ROWS), pl.ds(ROWS, RANK)]
    unit = (
        lax.broadcasted_iota(jnp.int32, (RANK, RANK), 0)
        == lax.broadcasted_iota(jnp.int32, (RANK, RANK), 1)
    ).astype(jnp.float32)

    def one_pass(index, carry):
        work[:, pl.ds(0, RANK)] = jnp.zeros((RANK, RANK), jnp.float32)
        work[:, pl.ds(RANK, RANK)] = unit

        for i in range(6):
            at = pl.ds(i * BLOCK, BLOCK)
            image = nn(high[at, pl.ds(0, ROWS)], basis[...]) + nn(low[at, pl.ds(0, ROWS)], basis[...])
            q[at, :] = image
            parts = split(image)
            line = basis[at, :].astype(jnp.float32).T.astype(jnp.bfloat16)
            work[:, pl.ds(0, RANK)] += (nn(line, parts[0]) + nn(line, parts[1])) + nn(line, parts[2])

        work[:, pl.ds(0, RANK)] = work[:, pl.ds(0, RANK)] * (1.0 / GRID)
        for p in range(4):
            top = 64 * p
            inverse = factor_inverse(work[pl.ds(top, 64), pl.ds(top, 64)], 64)
            panel = nn(inverse, work[pl.ds(top, 64), :], EXACT)
            work[pl.ds(top, 64), :] = panel
            if p < 3:
                rest = 256 - top - 64
                work[pl.ds(top + 64, rest), :] -= tn(panel[:, top + 64 : 256], panel, EXACT)
        solve = work[:, pl.ds(RANK, RANK)]

        @pl.when(index == PASSES - 1)
        def _():
            spread[...] = tn(xg[...], basis[...])
            own = spread[pl.ds(pl.multiple_of(core * SHARD_ROWS, 64), SHARD_ROWS), :]
            factor_ref[...] = nt(own, solve, EXACT)

        @pl.loop(0, 6)
        def _(i):
            at = pl.ds(pl.multiple_of(i * BLOCK, BLOCK), BLOCK)
            basis[at, :] = nt(q[at, :], solve, EXACT).astype(jnp.bfloat16)

        return carry

    lax.fori_loop(0, PASSES, one_pass, 0)
    final_ref[...] = basis[...]


def factors(high, low, xg):
    f32, bf16 = jnp.float32, jnp.bfloat16
    vmem = pl.BlockSpec(memory_space=pltpu.VMEM)
    return pl.pallas_call(
        factor_kernel,
        out_shape=(
            jax.ShapeDtypeStruct((SHARD_ROWS, RANK), f32),
            jax.ShapeDtypeStruct((ROWS, RANK), bf16),
        ),
        in_specs=[vmem, vmem, vmem],
        out_specs=(vmem, vmem),
        scratch_shapes=[
            pltpu.VMEM((ROWS, RANK), bf16),
            pltpu.VMEM((ROWS, RANK), f32),
            pltpu.VMEM((RANK, 2 * RANK), f32),
            pltpu.VMEM((CHIP_COLS, RANK), f32),
        ],
        compiler_params=pltpu.CompilerParams(vmem_limit_bytes=30 << 20),
        name="passes",
    )(high, low, xg)


def inner_gram(image_rows):
    return tn(image_rows, image_rows, EXACT)


def solve_right(lower_factor, image_rows):
    return lax.linalg.triangular_solve(
        lower_factor, image_rows, left_side=False, lower=True, transpose_a=True
    )


def refine(gram_matrix, previous, row_count):
    image_rows = nn(gram_matrix, previous, EXACT)
    lower_factor = jnp.linalg.cholesky(inner_gram(image_rows) / row_count)
    return solve_right(lower_factor, image_rows)


def factor_grams(final_band_lines):
    by_level = final_band_lines.reshape(LEVELS, -1)
    level_gram = jnp.dot(by_level, by_level.T, preferred_element_type=jnp.float32)
    by_member = (
        final_band_lines.reshape(LEVELS, MEMBERS, -1).transpose(1, 0, 2).reshape(MEMBERS, -1)
    )
    member_gram = jnp.dot(by_member, by_member.T, preferred_element_type=jnp.float32)
    return (member_gram, level_gram)


def on_device(outlook_array, earlier_location_basis, earlier_ensemble_basis, earlier_height_basis):
    high, low, slab = exchange(outlook_array, earlier_location_basis)
    factor, final = factors(high, low, slab)
    member_gram, level_gram = factor_grams(final)
    return (
        factor,
        refine(member_gram, earlier_ensemble_basis, MEMBERS),
        refine(level_gram, earlier_height_basis, LEVELS),
    )


def solution(mesh):
    in_specs = (P("ens", "space"), P("space", None), P(), P())
    out_specs = (P(("space", "ens"), None), P(), P())
    return jax.shard_map(
        on_device, mesh=mesh, in_specs=in_specs, out_specs=out_specs, check_vma=False
    )
```
